32 devices in a mesh: grp: 4 (over x, core), env: 8 (over z, y).
Axes of the slice: x: 2, y: 2, z: 4, core: 2. Of those that a mesh axis runs over, the one named last changes fastest.
Arguments:
- wavefunction: bfloat16 [8192, 1024], P('grp', 'env'), may hold values from -6 to 6
- left_tiles: bfloat16 [512, 128, 128], P(('grp', 'env')), may hold values from -0.5 to 0.5
- right_tiles: bfloat16 [26, 1024, 128], P(None, 'env'), may hold values from -0.5 to 0.5
- term_source: int32 [512], P('grp'), may hold values from 0 to 63
- term_target: int32 [512], P('grp'), may hold values from 0 to 63
- right_index: int32 [512], P('grp'), may hold values from 0 to 25
- term_sector: int32 [512, 1], P('grp'), may hold values from 0 to 31; in each aligned block of 16 rows (0 to 15, 16 to 31, ...) at most 4 rows name the same one
- column_sector: int32 [8], replicated, may hold values from 0 to 31
Outputs:
- applied: bfloat16 [8192, 1024], P('grp', 'env')
The draws below stay inside these ranges and needn't reach their ends.
Inputs may be any that keep to these rules, and one draw needn't show every extreme that they name: `term_sector`: within each aligned block of 16 terms (the terms of one device) no sector appears more than 4 times, and every sector appears somewhere.
All inputs are finite; a program needn't handle non-finite values.
Results may differ from the reference program's by a relative error of at most 0.009.
Values may be sent and summed in bfloat16 or wider, within the bound.
A program may use at most 64 MiB of HBM per device.

```python
import math
import jax
import jax.numpy as jnp
import numpy as np
from jax import lax

BLK = 128
NBLK = 64
NSEC = 32
NW = 26
MAXS = 4
TILES_DEV = 16
TG = 128
TERMS = 512
ROWS = 8192
COLS = 1024
SLOTS = 32
N_GRP = 4
N_ENV = 8


def set_ends(drawn, own_key, smallest, high):
    shape = drawn.shape
    place = [jax.random.randint(jax.random.fold_in(own_key, axis), (), 0, shape[axis]) for axis in range(len(shape))]
    drawn = drawn.at[tuple(place)].set(smallest)
    longest = shape.index(max(shape))
    place[longest] = (place[longest] + 1) % shape[longest]
    return drawn.at[tuple(place)].set(high)


def shard_levels(key, dims, cuts, smallest, high):
    gain, own = 1.0, jax.random.fold_in(key, 6)
    for position, parts in cuts:
        heights = jnp.exp(jax.random.uniform(jax.random.fold_in(own, position), (parts,), jnp.float32, smallest / len(cuts), high / len(cuts)))
        gain = gain * jnp.repeat(heights, dims[position] // parts).reshape([-1 if axis == position else 1 for axis in range(len(dims))])
    return gain


def assign_block(rng, own, number, rows, count, top, limit, lean):
    sequence = jax.random.permutation(rng, count)
    packed, common = load_shares(count, rows * top, limit, lean, True), load_shares(count, rows * top, limit, lean, False)
    places = jnp.arange(count)

    def named(tallies, turn):
        used = int((tallies > 0).sum())
        fixed = max(1, used // 4)
        passed = fixed + (places - fixed + turn * (used - fixed)) % max(1, count - fixed)
        return jnp.zeros((count,), jnp.int32).at[sequence[jnp.where(places < fixed, places, passed)]].set(jnp.asarray(tallies, jnp.int32))

    tallies = jnp.where(number % 4 == 0, named(packed, number // 4), named(common, number - number // 4 - 1))
    mixed = jax.random.permutation(jax.random.fold_in(own, 3), count)
    source_of, receiver = mixed[0:count // 2 * 2:2], mixed[1:count // 2 * 2:2]
    room = jnp.minimum(tallies[source_of] - 1, limit - tallies[receiver]) // 2
    room = jnp.where((source_of == sequence[0]) | (receiver == sequence[0]) | (tallies[receiver] == 0), 0, jnp.maximum(room, 0))
    passed = jax.random.randint(jax.random.fold_in(own, 4), (count // 2,), 0, 1 << 20) % (room + 1)
    tallies = tallies.at[source_of].add(-passed).at[receiver].add(passed)
    labels = jnp.searchsorted(jnp.cumsum(tallies), jnp.arange(rows * top), side="right").astype(jnp.int32)
    listing = labels.reshape(top, rows).T
    listing = listing[jax.random.permutation(jax.random.fold_in(own, 1), rows)]
    turn = jax.random.randint(jax.random.fold_in(own, 2), (rows, 1), 0, top)
    return jnp.take_along_axis(listing, (jnp.arange(top)[None, :] + turn) % top, axis=1)


def load_shares(count, total, most, skew, full):
    weights = [(1 << 20) // math.isqrt(standing ** skew) + 1 for standing in range(1, count + 1)]
    largest = most if full else min(most, max(-(-total // count), total * weights[0] // sum(weights)))
    least = 1 if total - largest >= count - 1 else 0
    holding, rest = [largest] + [least] * (count - 1), total - largest - least * (count - 1)
    while rest > 0:
        free = [i for i in range(1, count) if holding[i] < largest] or [i for i in range(1, count) if holding[i] < most]
        whole, left = sum([weights[i] for i in free]), rest
        for i in free:
            more = min(most - holding[i], max(1, left * weights[i] // whole), rest)
            holding[i] = holding[i] + more
            rest = rest - more
    return np.array(holding)


def centred(stream_key, shape, scale, most, split=(), held_as=jnp.bfloat16):
    level = shard_levels(stream_key, shape, split, -0.22, 0.18) if split else 1.0
    drawn = jax.random.normal(stream_key, shape, jnp.float32) * scale * level
    return jnp.minimum(jnp.maximum(drawn, -most), most).astype(held_as)


def setup_inputs(seed: int = 0) -> dict:
    key_list = jax.random.split(jax.random.key(seed), 9)
    wavefunction = centred(key_list[0], (ROWS, COLS), 1.0, 6.0, ((0, 4), (1, 8)))
    left_tiles = centred(key_list[1], (TERMS, BLK, BLK), BLK ** -0.5, 0.5, ((0, 32),))
    right_tiles = centred(key_list[2], (NW, COLS, BLK), BLK ** -0.5, 0.5, ((1, 8),))
    term_source = set_ends(jax.random.randint(key_list[3], (TERMS,), 0, NBLK), jax.random.fold_in(key_list[3], 1), 0, NBLK - 1).astype(jnp.int32)
    term_target = set_ends(jax.random.randint(key_list[4], (TERMS,), 0, NBLK), jax.random.fold_in(key_list[4], 1), 0, NBLK - 1).astype(jnp.int32)
    right_index = set_ends(jax.random.randint(key_list[5], (TERMS,), 0, NW), jax.random.fold_in(key_list[5], 1), 0, NW - 1).astype(jnp.int32)
    term_sector_keys = jax.random.split(jax.random.fold_in(key_list[6], 1), TERMS // TILES_DEV)
    term_sector_turns = jax.random.permutation(jax.random.fold_in(key_list[6], 3), TERMS // TILES_DEV)
    term_sector = jax.vmap(lambda own, number: assign_block(jax.random.fold_in(key_list[6], 2), own, number, TILES_DEV, NSEC, 1, MAXS, 2))(term_sector_keys, term_sector_turns).reshape((TERMS, 1))
    column_sector = set_ends(jax.random.randint(key_list[7], (N_ENV,), 0, NSEC), jax.random.fold_in(key_list[7], 1), 0, NSEC - 1).astype(jnp.int32)
    return {"wavefunction": wavefunction, "left_tiles": left_tiles, "right_tiles": right_tiles, "term_source": term_source, "term_target": term_target, "right_index": right_index, "term_sector": term_sector, "column_sector": column_sector}


def group_part(left_group, source_group, target_group, right_group, sector_group, wavefunction, right_tiles, column_sector):
    def one_column(column):
        wanted = column_sector[column]
        missing = (sector_group != wanted).astype(jnp.int32)
        ordering = jnp.argsort(missing, stable=True)[:SLOTS]
        kept_mask = (1 - missing[ordering]).astype(jnp.float32)
        columns = lax.dynamic_slice_in_dim(wavefunction, column * BLK, BLK, 1).reshape(NBLK, BLK, BLK)
        right_cols = lax.dynamic_slice_in_dim(right_tiles, column * BLK, BLK, 1)
        left_pick = left_group[ordering].astype(jnp.float32)
        source_blocks = columns[source_group[ordering]].astype(jnp.float32)
        block_product = jnp.einsum("kab,kbc->kac", left_pick, source_blocks, precision=lax.Precision.HIGHEST).astype(jnp.bfloat16)
        block_product = lax.optimization_barrier(block_product).astype(jnp.float32)
        right_pick = right_cols[right_group[ordering]].astype(jnp.float32)
        term_image = jnp.einsum("kac,kcd->kad", block_product, right_pick, precision=lax.Precision.HIGHEST)
        term_image = term_image * kept_mask[:, None, None]
        summed_rows = jnp.zeros((NBLK, BLK, BLK), jnp.float32).at[target_group[ordering]].add(term_image)
        return summed_rows.reshape(ROWS, BLK)

    pieces = lax.map(one_column, jnp.arange(N_ENV, dtype=jnp.int32))
    return jnp.transpose(pieces, (1, 0, 2)).reshape(ROWS, COLS).astype(jnp.bfloat16)


def reference(wavefunction, left_tiles, right_tiles, term_source, term_target, right_index, term_sector, column_sector):
    sectors = term_sector[:, 0]

    def one_group(running, group):
        first_term = group * TG

        def take_group(values):
            return lax.dynamic_slice_in_dim(values, first_term, TG, 0)

        group_partial = group_part(take_group(left_tiles), take_group(term_source), take_group(term_target), take_group(right_index), take_group(sectors), wavefunction, right_tiles, column_sector)
        return running + group_partial.astype(jnp.float32), None

    summed, ignored_out = lax.scan(one_group, jnp.zeros((ROWS, COLS), jnp.float32), jnp.arange(N_GRP, dtype=jnp.int32))
    return summed.astype(jnp.bfloat16)
```

```python
import functools

import jax
import jax.numpy as jnp
from jax import lax
from jax.experimental import pallas as pl
from jax.experimental.pallas import tpu as pltpu
from jax.sharding import PartitionSpec as P

MAXS = 4
MESH = pl.DeviceIdType.MESH


def remote(src, dst, send_sem, recv_sem, where):
    return pltpu.make_async_remote_copy(
        src_ref=src,
        dst_ref=dst,
        send_sem=send_sem,
        recv_sem=recv_sem,
        device_id=where,
        device_id_type=MESH,
    )


def exchange_kernel(
    ng,
    ne,
    meta_ref,
    meta_any,
    column_ref,
    wave_ref,
    left_ref,
    gathered_ref,
    tiles_ref,
    partner_meta_ref,
    slots_ref,
    outgoing,
    meta_two,
    a2a_send,
    a2a_recv,
    fwd_send,
    fwd_recv,
    ag_send,
    ag_recv,
    agf_send,
    agf_recv,
    own_send,
    own_recv,
    local_sem,
):
    g = lax.axis_index("grp")
    e = lax.axis_index("env")
    chips = ng // 2
    core = lax.rem(g, 2)
    chip = lax.div(g, 2)
    partner = chip * 2 + 1 - core
    tiles_dev = left_ref.shape[0]
    bpd = wave_ref.shape[0]
    tg = tiles_dev * ne

    barrier = pltpu.get_barrier_semaphore()

    def greet_env(d, c):
        pl.semaphore_signal(
            barrier, inc=1, device_id={"grp": g, "env": lax.rem(e + d, ne)}, device_id_type=MESH
        )
        return c

    def greet_chip(d, c):
        pl.semaphore_signal(
            barrier,
            inc=1,
            device_id={"grp": lax.rem(chip + d, chips) * 2 + core, "env": e},
            device_id_type=MESH,
        )
        return c

    lax.fori_loop(1, ne, greet_env, 0)
    lax.fori_loop(1, chips, greet_chip, 0)
    pl.semaphore_signal(barrier, inc=1, device_id={"grp": partner, "env": e}, device_id_type=MESH)

    def ranked(read, wanted):
        packed, weight, count = jnp.int32(0), jnp.int32(1), jnp.int32(0)
        for t in range(tiles_dev):
            hit = read(t) == wanted
            packed = packed + jnp.where(hit, t * weight, 0)
            weight = jnp.where(hit, weight * tiles_dev, weight)
            count = count + jnp.where(hit, 1, 0)
        picks = []
        for s in range(MAXS):
            picks.append(lax.rem(packed, tiles_dev))
            packed = lax.div(packed, tiles_dev)
        return picks, count

    def choose(c, carry):
        base = 3 * tg + e * tiles_dev
        picks, _ = ranked(lambda t: meta_ref[base + t], column_ref[c])
        for s in range(MAXS):
            outgoing[c, s] = left_ref[picks[s]]
        return carry

    lax.fori_loop(0, ne, choose, 0)

    pl.semaphore_wait(barrier, ne - 1 + chips)

    there = {"grp": partner, "env": e}

    def a2a(d):
        return remote(
            outgoing.at[lax.rem(e + d, ne)],
            tiles_ref.at[0, e],
            a2a_send.at[d],
            a2a_recv.at[d],
            {"grp": g, "env": lax.rem(e + d, ne)},
        )

    def a2a_in(d):
        src = lax.rem(e + ne - d, ne)
        return remote(
            outgoing.at[src],
            tiles_ref.at[0, src],
            a2a_send.at[d],
            a2a_recv.at[d],
            {"grp": g, "env": lax.rem(e + d, ne)},
        )

    def forward(d):
        src = lax.rem(e + ne - d, ne)
        return remote(
            tiles_ref.at[0, src], tiles_ref.at[1, src], fwd_send.at[d], fwd_recv.at[d], there
        )

    def ag(d):
        return remote(
            wave_ref,
            gathered_ref.at[g],
            ag_send.at[d],
            ag_recv.at[d],
            {"grp": lax.rem(chip + d, chips) * 2 + core, "env": e},
        )

    def ag_in(d):
        src = lax.rem(chip + chips - d, chips) * 2 + core
        return remote(
            wave_ref,
            gathered_ref.at[src],
            ag_send.at[d],
            ag_recv.at[d],
            {"grp": lax.rem(chip + d, chips) * 2 + core, "env": e},
        )

    def ag_forward(d):
        src = lax.rem(chip + chips - d, chips) * 2 + core
        return remote(
            gathered_ref.at[src], gathered_ref.at[src], agf_send.at[d], agf_recv.at[d], there
        )

    def ag_forward_in(d):
        src = lax.rem(chip + chips - d, chips) * 2 + 1 - core
        return remote(
            gathered_ref.at[src], gathered_ref.at[src], agf_send.at[d], agf_recv.at[d], there
        )

    def loop(low, high, act):
        def step(d, c):
            act(d)
            return c

        lax.fori_loop(low, high, step, 0)

    loop(1, ne, lambda d: a2a(d).start())
    loop(1, chips, lambda d: ag(d).start())
    own_meta = remote(meta_any, partner_meta_ref, own_send.at[0], own_recv.at[0], there)
    own_meta.start()
    own_wave = remote(wave_ref, gathered_ref.at[g], own_send.at[1], own_recv.at[1], there)
    own_wave.start()
    own_wave_in = remote(wave_ref, gathered_ref.at[partner], own_send.at[1], own_recv.at[1], there)
    own_tiles = remote(
        outgoing.at[e], tiles_ref.at[1, e], own_send.at[2], own_recv.at[2], there
    )
    own_tiles.start()
    keep_wave = pltpu.make_async_copy(wave_ref, gathered_ref.at[g], local_sem.at[0])
    keep_wave.start()
    keep_tiles = pltpu.make_async_copy(outgoing.at[e], tiles_ref.at[0, e], local_sem.at[1])
    keep_tiles.start()

    own_meta.wait_recv()
    fetch = pltpu.make_async_copy(partner_meta_ref, meta_two, local_sem.at[2])
    fetch.start()
    fetch.wait()
    wanted = column_ref[e]

    def list_slots(half, table):
        def block(b, carry):
            base = b * tiles_dev
            picks, count = ranked(lambda t: table[3 * tg + base + t], wanted)
            for s in range(MAXS):
                term = base + picks[s]
                target = table[tg + term]
                owner = lax.div(target, bpd)
                row = lax.div(owner, 2) * bpd + lax.rem(target, bpd)
                mine = (lax.rem(owner, 2) == core) & (count > s)
                place = (half * ne + b) * MAXS + s
                slots_ref[0, place] = jnp.where(mine, row, -1)
                slots_ref[1, place] = table[term]
                slots_ref[2, place] = table[2 * tg + term]
            return carry

        lax.fori_loop(0, ne, block, 0)

    list_slots(0, meta_ref)
    list_slots(1, meta_two)

    def pass_on(d):
        a2a_in(d).wait_recv()
        forward(d).start()

    def pass_wave(d):
        ag_in(d).wait_recv()
        ag_forward(d).start()

    half = 1 + ne // 2
    loop(1, half, pass_on)
    loop(1, chips, pass_wave)
    loop(half, ne, pass_on)

    loop(1, ne, lambda d: forward(d).wait_recv())
    loop(1, chips, lambda d: ag_forward_in(d).wait_recv())
    own_wave_in.wait_recv()
    own_tiles.wait_recv()
    keep_wave.wait()
    keep_tiles.wait()
    loop(1, ne, lambda d: a2a(d).wait_send())
    loop(1, ne, lambda d: forward(d).wait_send())
    loop(1, chips, lambda d: ag(d).wait_send())
    loop(1, chips, lambda d: ag_forward(d).wait_send())
    own_meta.wait_send()
    own_wave.wait_send()
    own_tiles.wait_send()


UNROLL = 4


def term_kernel(slots_ref, gathered_ref, tiles_ref, right_ref, out_ref, total, listed):
    rows = out_ref.shape[0]
    places = slots_ref.shape[1]
    total[...] = jnp.zeros_like(total)

    def collect(i, n):
        row = slots_ref[0, i]
        listed[0, n] = row
        listed[1, n] = slots_ref[1, i]
        listed[2, n] = slots_ref[2, i]
        listed[3, n] = i
        return n + jnp.where(row >= 0, 1, 0)

    n = lax.fori_loop(0, places, collect, jnp.int32(0))
    for u in range(UNROLL):
        listed[0, n + u] = rows
        listed[1, n + u] = 0
        listed[2, n + u] = 0
        listed[3, n + u] = 0

    def batch(i, carry):
        images = []
        for u in range(UNROLL):
            at = i * UNROLL + u
            product = jnp.dot(
                tiles_ref[listed[3, at]],
                gathered_ref[listed[1, at]],
                preferred_element_type=jnp.float32,
            ).astype(jnp.bfloat16)
            images.append(
                jnp.dot(product, right_ref[listed[2, at]], preferred_element_type=jnp.float32)
            )
        for u in range(UNROLL):
            row = listed[0, i * UNROLL + u]
            total[row] = total[row] + images[u]
        return carry

    lax.fori_loop(0, lax.div(n + UNROLL - 1, UNROLL), batch, 0)

    def finish(r, carry):
        out_ref[r] = total[r].astype(out_ref.dtype)
        return carry

    lax.fori_loop(0, rows, finish, 0)


CHUNKS = 4


def reduce_kernel(ng, part_ref, out_ref, landed, send_sem, recv_sem):
    g = lax.axis_index("grp")
    e = lax.axis_index("env")
    chips = ng // 2
    core = lax.rem(g, 2)
    chip = lax.div(g, 2)
    size = part_ref.shape[1] // CHUNKS

    barrier = pltpu.get_barrier_semaphore()
    for d in range(1, chips):
        to = lax.rem(chip + d, chips) * 2 + core
        pl.semaphore_signal(barrier, inc=1, device_id={"grp": to, "env": e}, device_id_type=MESH)
    pl.semaphore_wait(barrier, chips - 1)

    def move(c, d):
        to = lax.rem(chip + d, chips)
        piece = pl.ds(c * size, size)
        return remote(
            part_ref.at[to, piece],
            landed.at[d, piece],
            send_sem.at[c, d],
            recv_sem.at[c, d],
            {"grp": to * 2 + core, "env": e},
        )

    for c in range(CHUNKS):
        for d in range(1, chips):
            move(c, d).start()
    for c in range(CHUNKS):
        piece = pl.ds(c * size, size)
        summed = part_ref[chip, piece].astype(jnp.float32)
        for d in range(1, chips):
            move(c, d).wait_recv()
            summed = summed + landed[d, piece].astype(jnp.float32)
        out_ref[piece] = summed.astype(out_ref.dtype)
    for c in range(CHUNKS):
        for d in range(1, chips):
            move(c, d).wait_send()


def shards(
    wavefunction,
    left_tiles,
    right_tiles,
    term_source,
    term_target,
    right_index,
    term_sector,
    column_sector,
):
    tile = left_tiles.shape[1]
    tiles_dev = left_tiles.shape[0]
    ne = lax.axis_size("env")
    ng = lax.axis_size("grp")
    chips = ng // 2
    rows_dev = wavefunction.shape[0]
    bpd = rows_dev // tile
    meta = jnp.concatenate([term_source, term_target, right_index, term_sector[:, 0]])
    wave = wavefunction.reshape(bpd, tile, tile)
    bf16 = jnp.bfloat16
    vmem = pl.BlockSpec(memory_space=pltpu.VMEM)
    smem = pl.BlockSpec(memory_space=pltpu.SMEM)
    anywhere = pl.BlockSpec(memory_space=pl.ANY)
    places = 2 * ne * MAXS
    dma = pltpu.SemaphoreType.DMA

    gathered, tiles, _, slots = pl.pallas_call(
        functools.partial(exchange_kernel, ng, ne),
        out_shape=(
            jax.ShapeDtypeStruct((ng, bpd, tile, tile), bf16),
            jax.ShapeDtypeStruct((2, ne, MAXS, tile, tile), bf16),
            jax.ShapeDtypeStruct(meta.shape, jnp.int32),
            jax.ShapeDtypeStruct((3, places), jnp.int32),
        ),
        in_specs=[smem, anywhere, smem, vmem, vmem],
        out_specs=(anywhere, anywhere, anywhere, smem),
        scratch_shapes=[
            pltpu.VMEM((ne, MAXS, tile, tile), bf16),
            pltpu.SMEM(meta.shape, jnp.int32),
            dma((ne,)),
            dma((ne,)),
            dma((ne,)),
            dma((ne,)),
            dma((chips,)),
            dma((chips,)),
            dma((chips,)),
            dma((chips,)),
            dma((3,)),
            dma((3,)),
            dma((3,)),
        ],
        compiler_params=pltpu.CompilerParams(collective_id=0, has_side_effects=True),
        name="exchange",
    )(meta, meta, column_sector, wave, left_tiles)

    part = pl.pallas_call(
        term_kernel,
        out_shape=jax.ShapeDtypeStruct((chips * bpd, tile, tile), bf16),
        in_specs=[smem, vmem, vmem, vmem],
        out_specs=vmem,
        scratch_shapes=[
            pltpu.VMEM((chips * bpd + 1, tile, tile), jnp.float32),
            pltpu.SMEM((4, places + UNROLL), jnp.int32),
        ],
        name="terms",
    )(
        slots,
        gathered.reshape(ng * bpd, tile, tile),
        tiles.reshape(places, tile, tile),
        right_tiles,
    )

    return pl.pallas_call(
        functools.partial(reduce_kernel, ng),
        out_shape=jax.ShapeDtypeStruct((rows_dev, tile), bf16),
        in_specs=[vmem],
        out_specs=vmem,
        scratch_shapes=[
            pltpu.VMEM((chips, rows_dev, tile), bf16),
            dma((CHUNKS, chips)),
            dma((CHUNKS, chips)),
        ],
        compiler_params=pltpu.CompilerParams(collective_id=1, has_side_effects=True),
        name="reduce",
    )(part.reshape(chips, rows_dev, tile))


def solution(mesh):
    placed = (
        P("grp", "env"),
        P(("grp", "env"), None, None),
        P(None, "env", None),
        P("grp"),
        P("grp"),
        P("grp"),
        P("grp", None),
        P(),
    )
    return jax.shard_map(
        shards, mesh=mesh, in_specs=placed, out_specs=P("grp", "env"), check_vma=False
    )
```

```python
import functools

import jax
import jax.numpy as jnp
from jax import lax
from jax.experimental import pallas as pl
from jax.experimental.pallas import tpu as pltpu
from jax.sharding import PartitionSpec as P

MAXS = 4
MESH = pl.DeviceIdType.MESH


def remote(src, dst, send_sem, recv_sem, where):
    return pltpu.make_async_remote_copy(
        src_ref=src,
        dst_ref=dst,
        send_sem=send_sem,
        recv_sem=recv_sem,
        device_id=where,
        device_id_type=MESH,
    )


def exchange_kernel(
    ng,
    ne,
    src_ref,
    tgt_ref,
    mpo_ref,
    sec_ref,
    src_any,
    tgt_any,
    mpo_any,
    sec_any,
    column_ref,
    wave_ref,
    left_ref,
    gathered_ref,
    tiles_ref,
    src_far,
    tgt_far,
    mpo_far,
    sec_far,
    slots_ref,
    outgoing,
    src_two,
    tgt_two,
    mpo_two,
    sec_two,
    a2a_send,
    a2a_recv,
    fwd_send,
    fwd_recv,
    ag_send,
    ag_recv,
    agf_send,
    agf_recv,
    own_send,
    own_recv,
    local_sem,
):
    g = lax.axis_index("grp")
    e = lax.axis_index("env")
    chips = ng // 2
    core = lax.rem(g, 2)
    chip = lax.div(g, 2)
    partner = chip * 2 + 1 - core

    def mate(d):
        other, bit = jnp.int32(0), 1
        while bit < ne:
            ours, step = lax.rem(lax.div(e, bit), 2), lax.rem(lax.div(d, bit), 2)
            other = other + lax.rem(ours + step, 2) * bit
            bit *= 2
        return other

    tiles_dev = left_ref.shape[0]
    bpd = wave_ref.shape[0]

    barrier = pltpu.get_barrier_semaphore()

    def greet_env(d, c):
        pl.semaphore_signal(
            barrier, inc=1, device_id={"grp": g, "env": mate(d)}, device_id_type=MESH
        )
        return c

    def greet_chip(d, c):
        pl.semaphore_signal(
            barrier,
            inc=1,
            device_id={"grp": lax.rem(chip + d, chips) * 2 + core, "env": e},
            device_id_type=MESH,
        )
        return c

    lax.fori_loop(1, ne, greet_env, 0)
    lax.fori_loop(1, chips, greet_chip, 0)
    pl.semaphore_signal(barrier, inc=1, device_id={"grp": partner, "env": e}, device_id_type=MESH)

    def ranked(read, wanted):
        packed, weight, count = jnp.int32(0), jnp.int32(1), jnp.int32(0)
        for t in range(tiles_dev):
            hit = read(t) == wanted
            packed = packed + jnp.where(hit, t * weight, 0)
            weight = jnp.where(hit, weight * tiles_dev, weight)
            count = count + jnp.where(hit, 1, 0)
        picks = []
        for s in range(MAXS):
            picks.append(lax.rem(packed, tiles_dev))
            packed = lax.div(packed, tiles_dev)
        return picks, count

    def choose(c, carry):
        base = e * tiles_dev
        picks, _ = ranked(lambda t: sec_ref[base + t], column_ref[c])
        for s in range(MAXS):
            outgoing[c, s] = left_ref[picks[s]]
        return carry

    lax.fori_loop(0, ne, choose, 0)

    pl.semaphore_wait(barrier, ne - 1 + chips)

    there = {"grp": partner, "env": e}

    def a2a(d):
        return remote(
            outgoing.at[mate(d)],
            tiles_ref.at[0, e],
            a2a_send.at[d],
            a2a_recv.at[d],
            {"grp": g, "env": mate(d)},
        )

    def a2a_in(d):
        src = mate(d)
        return remote(
            outgoing.at[src],
            tiles_ref.at[0, src],
            a2a_send.at[d],
            a2a_recv.at[d],
            {"grp": g, "env": mate(d)},
        )

    def forward(d):
        src = mate(d)
        return remote(
            tiles_ref.at[0, src], tiles_ref.at[1, src], fwd_send.at[d], fwd_recv.at[d], there
        )

    def ag(d):
        return remote(
            wave_ref,
            gathered_ref.at[g],
            ag_send.at[d],
            ag_recv.at[d],
            {"grp": lax.rem(chip + d, chips) * 2 + core, "env": e},
        )

    def ag_in(d):
        src = lax.rem(chip + chips - d, chips) * 2 + core
        return remote(
            wave_ref,
            gathered_ref.at[src],
            ag_send.at[d],
            ag_recv.at[d],
            {"grp": lax.rem(chip + d, chips) * 2 + core, "env": e},
        )

    def ag_forward(d):
        src = lax.rem(chip + chips - d, chips) * 2 + core
        return remote(
            gathered_ref.at[src], gathered_ref.at[src], agf_send.at[d], agf_recv.at[d], there
        )

    def ag_forward_in(d):
        src = lax.rem(chip + chips - d, chips) * 2 + 1 - core
        return remote(
            gathered_ref.at[src], gathered_ref.at[src], agf_send.at[d], agf_recv.at[d], there
        )

    def loop(low, high, act):
        def step(d, c):
            act(d)
            return c

        lax.fori_loop(low, high, step, 0)

    loop(1, ne, lambda d: a2a(d).start())
    loop(1, chips, lambda d: ag(d).start())
    far = (src_far, tgt_far, mpo_far, sec_far)
    own_meta = [
        remote(mine, theirs, own_send.at[3 + i], own_recv.at[3 + i], there)
        for i, (mine, theirs) in enumerate(zip((src_any, tgt_any, mpo_any, sec_any), far))
    ]
    for copy in own_meta:
        copy.start()
    own_wave = remote(wave_ref, gathered_ref.at[g], own_send.at[1], own_recv.at[1], there)
    own_wave.start()
    own_wave_in = remote(wave_ref, gathered_ref.at[partner], own_send.at[1], own_recv.at[1], there)
    own_tiles = remote(
        outgoing.at[e], tiles_ref.at[1, e], own_send.at[2], own_recv.at[2], there
    )
    own_tiles.start()
    keep_wave = pltpu.make_async_copy(wave_ref, gathered_ref.at[g], local_sem.at[0])
    keep_wave.start()
    keep_tiles = pltpu.make_async_copy(outgoing.at[e], tiles_ref.at[0, e], local_sem.at[1])
    keep_tiles.start()

    two = (src_two, tgt_two, mpo_two, sec_two)
    fetches = []
    for i in range(4):
        own_meta[i].wait_recv()
        fetches.append(pltpu.make_async_copy(far[i], two[i], local_sem.at[2 + i]))
        fetches[i].start()
    for fetch in fetches:
        fetch.wait()
    wanted = column_ref[e]

    def list_slots(half, source, goal, mpo, sector):
        def block(b, carry):
            base = b * tiles_dev
            picks, count = ranked(lambda t: sector[base + t], wanted)
            for s in range(MAXS):
                term = base + picks[s]
                target = goal[term]
                owner = lax.div(target, bpd)
                row = lax.rem(lax.div(owner, 2) + chips - chip, chips) * bpd + lax.rem(target, bpd)
                mine = (lax.rem(owner, 2) == core) & (count > s)
                place = (half * ne + b) * MAXS + s
                slots_ref[0, place] = jnp.where(mine, row, -1)
                slots_ref[1, place] = source[term]
                slots_ref[2, place] = mpo[term]
            return carry

        lax.fori_loop(0, ne, block, 0)

    list_slots(0, src_ref, tgt_ref, mpo_ref, sec_ref)
    list_slots(1, *two)

    def pass_on(d):
        a2a_in(d).wait_recv()
        forward(d).start()

    def pass_wave(d):
        ag_in(d).wait_recv()
        ag_forward(d).start()

    half = 1 + ne // 2
    loop(1, half, pass_on)
    loop(1, chips, pass_wave)
    loop(half, ne, pass_on)

    loop(1, ne, lambda d: forward(d).wait_recv())
    loop(1, chips, lambda d: ag_forward_in(d).wait_recv())
    own_wave_in.wait_recv()
    own_tiles.wait_recv()
    keep_wave.wait()
    keep_tiles.wait()
    loop(1, ne, lambda d: a2a(d).wait_send())
    loop(1, ne, lambda d: forward(d).wait_send())
    loop(1, chips, lambda d: ag(d).wait_send())
    loop(1, chips, lambda d: ag_forward(d).wait_send())
    for copy in own_meta:
        copy.wait_send()
    own_wave.wait_send()
    own_tiles.wait_send()


UNROLL = 4


def term_kernel(slots_ref, gathered_ref, tiles_ref, right_ref, own_ref, away_ref, total, listed):
    here = own_ref.shape[0]
    rows = here + away_ref.shape[0]
    places = slots_ref.shape[1]
    total[...] = jnp.zeros_like(total)

    def collect(i, n):
        row = slots_ref[0, i]
        listed[0, n] = row
        listed[1, n] = slots_ref[1, i]
        listed[2, n] = slots_ref[2, i]
        listed[3, n] = i
        return n + jnp.where(row >= 0, 1, 0)

    n = lax.fori_loop(0, places, collect, jnp.int32(0))
    for u in range(UNROLL):
        listed[0, n + u] = rows
        listed[1, n + u] = 0
        listed[2, n + u] = 0
        listed[3, n + u] = 0

    def batch(i, carry):
        images = []
        for u in range(UNROLL):
            at = i * UNROLL + u
            product = jnp.dot(
                tiles_ref[listed[3, at]],
                gathered_ref[listed[1, at]],
                preferred_element_type=jnp.float32,
            ).astype(jnp.bfloat16)
            images.append(
                jnp.dot(product, right_ref[listed[2, at]], preferred_element_type=jnp.float32)
            )
        for u in range(UNROLL):
            row = listed[0, i * UNROLL + u]
            total[row] = total[row] + images[u]
        return carry

    lax.fori_loop(0, lax.div(n + UNROLL - 1, UNROLL), batch, 0)

    def keep(r, carry):
        own_ref[r] = total[r].astype(own_ref.dtype)
        return carry

    def hand_out(r, carry):
        away_ref[r] = total[here + r].astype(away_ref.dtype)
        return carry

    lax.fori_loop(0, here, keep, 0)
    lax.fori_loop(0, rows - here, hand_out, 0)


def reduce_kernel(ng, away_ref, landed_ref, send_sem, recv_sem):
    g = lax.axis_index("grp")
    e = lax.axis_index("env")
    chips = ng // 2
    core = lax.rem(g, 2)
    chip = lax.div(g, 2)

    def there(d):
        return {"grp": lax.rem(chip + d, chips) * 2 + core, "env": e}

    barrier = pltpu.get_barrier_semaphore()
    for d in range(1, chips):
        pl.semaphore_signal(barrier, inc=1, device_id=there(d), device_id_type=MESH)
    pl.semaphore_wait(barrier, chips - 1)

    moves = [
        remote(
            away_ref.at[d - 1], landed_ref.at[d - 1], send_sem.at[d], recv_sem.at[d], there(d)
        )
        for d in range(1, chips)
    ]
    for move in moves:
        move.start()
    for move in moves:
        move.wait_recv()
    for move in moves:
        move.wait_send()


def shards(
    wavefunction,
    left_tiles,
    right_tiles,
    term_source,
    term_target,
    right_index,
    term_sector,
    column_sector,
):
    tile = left_tiles.shape[1]
    tiles_dev = left_tiles.shape[0]
    ne = lax.axis_size("env")
    ng = lax.axis_size("grp")
    chips = ng // 2
    rows_dev = wavefunction.shape[0]
    bpd = rows_dev // tile
    meta = (term_source, term_target, right_index, term_sector[:, 0])
    listing = jax.ShapeDtypeStruct(term_source.shape, jnp.int32)
    tile_bytes = tile * tile * 2
    spare = 4 << 20
    wave = wavefunction.reshape(bpd, tile, tile)
    bf16 = jnp.bfloat16
    vmem = pl.BlockSpec(memory_space=pltpu.VMEM)
    smem = pl.BlockSpec(memory_space=pltpu.SMEM)
    anywhere = pl.BlockSpec(memory_space=pl.ANY)
    places = 2 * ne * MAXS
    dma = pltpu.SemaphoreType.DMA

    gathered, tiles, *_, slots = pl.pallas_call(
        functools.partial(exchange_kernel, ng, ne),
        out_shape=(
            jax.ShapeDtypeStruct((ng, bpd, tile, tile), bf16),
            jax.ShapeDtypeStruct((2, ne, MAXS, tile, tile), bf16),
            listing,
            listing,
            listing,
            listing,
            jax.ShapeDtypeStruct((3, places), jnp.int32),
        ),
        in_specs=[smem] * 4 + [anywhere] * 4 + [smem, vmem, vmem],
        out_specs=(anywhere,) * 6 + (smem,),
        scratch_shapes=[
            pltpu.VMEM((ne, MAXS, tile, tile), bf16),
            *[pltpu.SMEM(listing.shape, jnp.int32) for _ in range(4)],
            dma((ne,)),
            dma((ne,)),
            dma((ne,)),
            dma((ne,)),
            dma((chips,)),
            dma((chips,)),
            dma((chips,)),
            dma((chips,)),
            dma((7,)),
            dma((7,)),
            dma((6,)),
        ],
        compiler_params=pltpu.CompilerParams(
            collective_id=0,
            has_side_effects=True,
            vmem_limit_bytes=spare + tile_bytes * (bpd + tiles_dev + ne * MAXS),
        ),
        name="exchange",
    )(*meta, *meta, column_sector, wave, left_tiles)

    own, away = pl.pallas_call(
        term_kernel,
        out_shape=(
            jax.ShapeDtypeStruct((bpd, tile, tile), bf16),
            jax.ShapeDtypeStruct(((chips - 1) * bpd, tile, tile), bf16),
        ),
        in_specs=[smem, vmem, vmem, vmem],
        out_specs=(vmem, vmem),
        scratch_shapes=[
            pltpu.VMEM((chips * bpd + 1, tile, tile), jnp.float32),
            pltpu.SMEM((4, places + UNROLL), jnp.int32),
        ],
        compiler_params=pltpu.CompilerParams(
            vmem_limit_bytes=spare
            + tile_bytes * (ng * bpd + places + right_tiles.shape[0] + 3 * chips * bpd + 2)
        ),
        name="terms",
    )(
        slots,
        gathered.reshape(ng * bpd, tile, tile),
        tiles.reshape(places, tile, tile),
        right_tiles,
    )

    landed = pl.pallas_call(
        functools.partial(reduce_kernel, ng),
        out_shape=jax.ShapeDtypeStruct((chips - 1, rows_dev, tile), bf16),
        in_specs=[anywhere],
        out_specs=anywhere,
        scratch_shapes=[dma((chips,)), dma((chips,))],
        compiler_params=pltpu.CompilerParams(
            collective_id=1, has_side_effects=True, vmem_limit_bytes=spare
        ),
        name="reduce",
    )(away.reshape(chips - 1, rows_dev, tile))
    summed = own.reshape(rows_dev, tile).astype(jnp.float32)
    for d in range(chips - 1):
        summed = summed + landed[d].astype(jnp.float32)
    return summed.astype(bf16)


def solution(mesh):
    placed = (
        P("grp", "env"),
        P(("grp", "env"), None, None),
        P(None, "env", None),
        P("grp"),
        P("grp"),
        P("grp"),
        P("grp", None),
        P(),
    )
    return jax.shard_map(
        shards, mesh=mesh, in_specs=placed, out_specs=P("grp", "env"), check_vma=False
    )
```

```python
import functools

import jax
import jax.numpy as jnp
from jax import lax
from jax.experimental import pallas as pl
from jax.experimental.pallas import tpu as pltpu
from jax.sharding import PartitionSpec as P

MAXS = 4
MESH = pl.DeviceIdType.MESH


def remote(src, dst, send_sem, recv_sem, where):
    return pltpu.make_async_remote_copy(
        src_ref=src,
        dst_ref=dst,
        send_sem=send_sem,
        recv_sem=recv_sem,
        device_id=where,
        device_id_type=MESH,
    )


def exchange_kernel(
    ng,
    ne,
    src_any,
    tgt_any,
    mpo_any,
    sec_any,
    column_any,
    wave_ref,
    left_any,
    right_any,
    gathered_ref,
    tiles_ref,
    right_ref,
    src_far,
    tgt_far,
    mpo_far,
    sec_far,
    slots_ref,
    outgoing,
    left_ref,
    src_ref,
    tgt_ref,
    mpo_ref,
    sec_ref,
    column_ref,
    src_two,
    tgt_two,
    mpo_two,
    sec_two,
    a2a_send,
    a2a_recv,
    fwd_send,
    fwd_recv,
    ag_send,
    ag_recv,
    agf_send,
    agf_recv,
    own_send,
    own_recv,
    local_sem,
):
    g = lax.axis_index("grp")
    e = lax.axis_index("env")
    chips = ng // 2
    core = lax.rem(g, 2)
    chip = lax.div(g, 2)
    partner = chip * 2 + 1 - core

    def mate(d):
        other, bit = jnp.int32(0), 1
        while bit < ne:
            ours, step = lax.rem(lax.div(e, bit), 2), lax.rem(lax.div(d, bit), 2)
            other = other + lax.rem(ours + step, 2) * bit
            bit *= 2
        return other

    tiles_dev = left_ref.shape[0]
    bpd = wave_ref.shape[0]

    starts = (
        (sec_any, sec_ref),
        (column_any, column_ref),
        (left_any, left_ref),
        (src_any, src_ref),
        (tgt_any, tgt_ref),
        (mpo_any, mpo_ref),
        (right_any, right_ref),
    )
    loads = [
        pltpu.make_async_copy(a, b, local_sem.at[6 + i]) for i, (a, b) in enumerate(starts)
    ]
    for load in loads[:3]:
        load.start()

    barrier = pltpu.get_barrier_semaphore()

    def greet_env(d, c):
        pl.semaphore_signal(
            barrier, inc=1, device_id={"grp": g, "env": mate(d)}, device_id_type=MESH
        )
        return c

    def greet_chip(d, c):
        pl.semaphore_signal(
            barrier,
            inc=1,
            device_id={"grp": lax.rem(chip + d, chips) * 2 + core, "env": e},
            device_id_type=MESH,
        )
        return c

    lax.fori_loop(1, ne, greet_env, 0)
    lax.fori_loop(1, chips, greet_chip, 0)
    pl.semaphore_signal(barrier, inc=1, device_id={"grp": partner, "env": e}, device_id_type=MESH)

    def ranked(read, wanted):
        packed, weight, count = jnp.int32(0), jnp.int32(1), jnp.int32(0)
        for t in range(tiles_dev):
            hit = read(t) == wanted
            packed = packed + jnp.where(hit, t * weight, 0)
            weight = jnp.where(hit, weight * tiles_dev, weight)
            count = count + jnp.where(hit, 1, 0)
        picks = []
        for s in range(MAXS):
            picks.append(lax.rem(packed, tiles_dev))
            packed = lax.div(packed, tiles_dev)
        return picks, count

    def choose(c, carry):
        base = e * tiles_dev
        picks, _ = ranked(lambda t: sec_ref[base + t], column_ref[c])
        for s in range(MAXS):
            outgoing[c, s] = left_ref[picks[s]]
        return carry

    for load in loads[:3]:
        load.wait()
    lax.fori_loop(0, ne, choose, 0)

    pl.semaphore_wait(barrier, ne - 1 + chips)

    there = {"grp": partner, "env": e}

    def a2a(d):
        return remote(
            outgoing.at[mate(d)],
            tiles_ref.at[0, e],
            a2a_send.at[d],
            a2a_recv.at[d],
            {"grp": g, "env": mate(d)},
        )

    def a2a_in(d):
        src = mate(d)
        return remote(
            outgoing.at[src],
            tiles_ref.at[0, src],
            a2a_send.at[d],
            a2a_recv.at[d],
            {"grp": g, "env": mate(d)},
        )

    def forward(d):
        src = mate(d)
        return remote(
            tiles_ref.at[0, src], tiles_ref.at[1, src], fwd_send.at[d], fwd_recv.at[d], there
        )

    def ag(d):
        return remote(
            wave_ref,
            gathered_ref.at[g],
            ag_send.at[d],
            ag_recv.at[d],
            {"grp": lax.rem(chip + d, chips) * 2 + core, "env": e},
        )

    def ag_in(d):
        src = lax.rem(chip + chips - d, chips) * 2 + core
        return remote(
            wave_ref,
            gathered_ref.at[src],
            ag_send.at[d],
            ag_recv.at[d],
            {"grp": lax.rem(chip + d, chips) * 2 + core, "env": e},
        )

    def ag_forward(d):
        src = lax.rem(chip + chips - d, chips) * 2 + core
        return remote(
            gathered_ref.at[src], gathered_ref.at[src], agf_send.at[d], agf_recv.at[d], there
        )

    def ag_forward_in(d):
        src = lax.rem(chip + chips - d, chips) * 2 + 1 - core
        return remote(
            gathered_ref.at[src], gathered_ref.at[src], agf_send.at[d], agf_recv.at[d], there
        )

    def loop(low, high, act):
        def step(d, c):
            act(d)
            return c

        lax.fori_loop(low, high, step, 0)

    loop(1, ne, lambda d: a2a(d).start())
    loop(1, chips, lambda d: ag(d).start())
    far = (src_far, tgt_far, mpo_far, sec_far)
    own_meta = [
        remote(mine, theirs, own_send.at[3 + i], own_recv.at[3 + i], there)
        for i, (mine, theirs) in enumerate(zip((src_any, tgt_any, mpo_any, sec_any), far))
    ]
    for copy in own_meta:
        copy.start()
    own_wave = remote(wave_ref, gathered_ref.at[g], own_send.at[1], own_recv.at[1], there)
    own_wave.start()
    own_wave_in = remote(wave_ref, gathered_ref.at[partner], own_send.at[1], own_recv.at[1], there)
    own_tiles = remote(
        outgoing.at[e], tiles_ref.at[1, e], own_send.at[2], own_recv.at[2], there
    )
    own_tiles.start()
    keep_wave = pltpu.make_async_copy(wave_ref, gathered_ref.at[g], local_sem.at[0])
    keep_wave.start()
    keep_tiles = pltpu.make_async_copy(outgoing.at[e], tiles_ref.at[0, e], local_sem.at[1])
    keep_tiles.start()

    for load in loads[3:]:
        load.start()
    two = (src_two, tgt_two, mpo_two, sec_two)
    fetches = []
    for i in range(4):
        own_meta[i].wait_recv()
        fetches.append(pltpu.make_async_copy(far[i], two[i], local_sem.at[2 + i]))
        fetches[i].start()
    for fetch in fetches:
        fetch.wait()
    for load in loads[3:6]:
        load.wait()
    wanted = column_ref[e]

    def list_slots(half, source, goal, mpo, sector):
        def block(b, carry):
            base = b * tiles_dev
            picks, count = ranked(lambda t: sector[base + t], wanted)
            for s in range(MAXS):
                term = base + picks[s]
                target = goal[term]
                owner = lax.div(target, bpd)
                row = lax.rem(lax.div(owner, 2) + chips - chip, chips) * bpd + lax.rem(target, bpd)
                mine = (lax.rem(owner, 2) == core) & (count > s)
                place = (half * ne + b) * MAXS + s
                slots_ref[0, place] = jnp.where(mine, row, -1)
                slots_ref[1, place] = source[term]
                slots_ref[2, place] = mpo[term]
            return carry

        lax.fori_loop(0, ne, block, 0)

    list_slots(0, src_ref, tgt_ref, mpo_ref, sec_ref)
    list_slots(1, *two)

    def pass_on(d):
        a2a_in(d).wait_recv()
        forward(d).start()

    def pass_wave(d):
        ag_in(d).wait_recv()
        ag_forward(d).start()

    half = 1 + ne // 2
    loop(1, half, pass_on)
    loop(1, chips, pass_wave)
    loop(half, ne, pass_on)

    loop(1, ne, lambda d: forward(d).wait_recv())
    loop(1, chips, lambda d: ag_forward_in(d).wait_recv())
    own_wave_in.wait_recv()
    own_tiles.wait_recv()
    keep_wave.wait()
    loads[6].wait()
    keep_tiles.wait()
    loop(1, ne, lambda d: a2a(d).wait_send())
    loop(1, ne, lambda d: forward(d).wait_send())
    loop(1, chips, lambda d: ag(d).wait_send())
    loop(1, chips, lambda d: ag_forward(d).wait_send())
    for copy in own_meta:
        copy.wait_send()
    own_wave.wait_send()
    own_tiles.wait_send()


UNROLL = 4


def term_kernel(slots_ref, gathered_ref, tiles_ref, right_ref, own_ref, away_ref, total, listed):
    here = own_ref.shape[0]
    rows = here + away_ref.shape[0]
    places = slots_ref.shape[1]
    total[...] = jnp.zeros_like(total)

    def collect(i, n):
        row = slots_ref[0, i]
        listed[0, n] = row
        listed[1, n] = slots_ref[1, i]
        listed[2, n] = slots_ref[2, i]
        listed[3, n] = i
        return n + jnp.where(row >= 0, 1, 0)

    n = lax.fori_loop(0, places, collect, jnp.int32(0))
    for u in range(UNROLL):
        listed[0, n + u] = rows
        listed[1, n + u] = 0
        listed[2, n + u] = 0
        listed[3, n + u] = 0

    def batch(i, carry):
        images = []
        for u in range(UNROLL):
            at = i * UNROLL + u
            product = jnp.dot(
                tiles_ref[listed[3, at]],
                gathered_ref[listed[1, at]],
                preferred_element_type=jnp.float32,
            ).astype(jnp.bfloat16)
            images.append(
                jnp.dot(product, right_ref[listed[2, at]], preferred_element_type=jnp.float32)
            )
        for u in range(UNROLL):
            row = listed[0, i * UNROLL + u]
            total[row] = total[row] + images[u]
        return carry

    lax.fori_loop(0, lax.div(n + UNROLL - 1, UNROLL), batch, 0)

    def keep(r, carry):
        own_ref[r] = total[r].astype(own_ref.dtype)
        return carry

    def hand_out(r, carry):
        away_ref[r] = total[here + r].astype(away_ref.dtype)
        return carry

    lax.fori_loop(0, here, keep, 0)
    lax.fori_loop(0, rows - here, hand_out, 0)


def reduce_kernel(ng, away_ref, landed_ref, send_sem, recv_sem):
    g = lax.axis_index("grp")
    e = lax.axis_index("env")
    chips = ng // 2
    core = lax.rem(g, 2)
    chip = lax.div(g, 2)

    def there(d):
        return {"grp": lax.rem(chip + d, chips) * 2 + core, "env": e}

    barrier = pltpu.get_barrier_semaphore()
    for d in range(1, chips):
        pl.semaphore_signal(barrier, inc=1, device_id=there(d), device_id_type=MESH)
    pl.semaphore_wait(barrier, chips - 1)

    moves = [
        remote(
            away_ref.at[d - 1], landed_ref.at[d - 1], send_sem.at[d], recv_sem.at[d], there(d)
        )
        for d in range(1, chips)
    ]
    for move in moves:
        move.start()
    for move in moves:
        move.wait_recv()
    for move in moves:
        move.wait_send()


def shards(
    wavefunction,
    left_tiles,
    right_tiles,
    term_source,
    term_target,
    right_index,
    term_sector,
    column_sector,
):
    tile = left_tiles.shape[1]
    tiles_dev = left_tiles.shape[0]
    ne = lax.axis_size("env")
    ng = lax.axis_size("grp")
    chips = ng // 2
    rows_dev = wavefunction.shape[0]
    bpd = rows_dev // tile
    meta = (term_source, term_target, right_index, term_sector[:, 0])
    listing = jax.ShapeDtypeStruct(term_source.shape, jnp.int32)
    tile_bytes = tile * tile * 2
    spare = 4 << 20
    wave = wavefunction.reshape(bpd, tile, tile)
    bf16 = jnp.bfloat16
    vmem = pl.BlockSpec(memory_space=pltpu.VMEM)
    smem = pl.BlockSpec(memory_space=pltpu.SMEM)
    hbm = pl.BlockSpec(memory_space=pltpu.HBM)
    anywhere = pl.BlockSpec(memory_space=pl.ANY)
    places = 2 * ne * MAXS
    dma = pltpu.SemaphoreType.DMA

    operands = (*meta, column_sector, wave, left_tiles, right_tiles)
    gathered, tiles, right_held, *_, slots = pl.pallas_call(
        functools.partial(exchange_kernel, ng, ne),
        out_shape=(
            jax.ShapeDtypeStruct((ng, bpd, tile, tile), bf16),
            jax.ShapeDtypeStruct((2, ne, MAXS, tile, tile), bf16),
            jax.ShapeDtypeStruct(right_tiles.shape, bf16),
            listing,
            listing,
            listing,
            listing,
            jax.ShapeDtypeStruct((3, places), jnp.int32),
        ),
        in_specs=[hbm] * 8,
        out_specs=(anywhere,) * 7 + (smem,),
        scratch_shapes=[
            pltpu.VMEM((ne, MAXS, tile, tile), bf16),
            pltpu.VMEM(left_tiles.shape, bf16),
            *[pltpu.SMEM(listing.shape, jnp.int32) for _ in range(4)],
            pltpu.SMEM(column_sector.shape, jnp.int32),
            *[pltpu.SMEM(listing.shape, jnp.int32) for _ in range(4)],
            dma((ne,)),
            dma((ne,)),
            dma((ne,)),
            dma((ne,)),
            dma((chips,)),
            dma((chips,)),
            dma((chips,)),
            dma((chips,)),
            dma((7,)),
            dma((7,)),
            dma((13,)),
        ],
        compiler_params=pltpu.CompilerParams(
            collective_id=0,
            has_side_effects=True,
            vmem_limit_bytes=spare + tile_bytes * (tiles_dev + ne * MAXS),
        ),
        name="exchange",
    )(*[pltpu.with_memory_space_constraint(a, pltpu.HBM) for a in operands])

    own, away = pl.pallas_call(
        term_kernel,
        out_shape=(
            jax.ShapeDtypeStruct((bpd, tile, tile), bf16),
            jax.ShapeDtypeStruct(((chips - 1) * bpd, tile, tile), bf16),
        ),
        in_specs=[smem, vmem, vmem, vmem],
        out_specs=(vmem, vmem),
        scratch_shapes=[
            pltpu.VMEM((chips * bpd + 1, tile, tile), jnp.float32),
            pltpu.SMEM((4, places + UNROLL), jnp.int32),
        ],
        compiler_params=pltpu.CompilerParams(
            vmem_limit_bytes=spare
            + tile_bytes * (ng * bpd + places + right_tiles.shape[0] + 3 * chips * bpd + 2)
        ),
        name="terms",
    )(
        slots,
        gathered.reshape(ng * bpd, tile, tile),
        tiles.reshape(places, tile, tile),
        right_held,
    )

    landed = pl.pallas_call(
        functools.partial(reduce_kernel, ng),
        out_shape=jax.ShapeDtypeStruct((chips - 1, rows_dev, tile), bf16),
        in_specs=[anywhere],
        out_specs=anywhere,
        scratch_shapes=[dma((chips,)), dma((chips,))],
        compiler_params=pltpu.CompilerParams(
            collective_id=1, has_side_effects=True, vmem_limit_bytes=spare
        ),
        name="reduce",
    )(away.reshape(chips - 1, rows_dev, tile))
    summed = own.reshape(rows_dev, tile).astype(jnp.float32)
    for d in range(chips - 1):
        summed = summed + landed[d].astype(jnp.float32)
    return summed.astype(bf16)


def solution(mesh):
    placed = (
        P("grp", "env"),
        P(("grp", "env"), None, None),
        P(None, "env", None),
        P("grp"),
        P("grp"),
        P("grp"),
        P("grp", None),
        P(),
    )
    return jax.shard_map(
        shards, mesh=mesh, in_specs=placed, out_specs=P("grp", "env"), check_vma=False
    )
```

```python
import functools

import jax
import jax.numpy as jnp
from jax import lax
from jax.experimental import pallas as pl
from jax.experimental.pallas import tpu as pltpu
from jax.sharding import PartitionSpec as P

MAXS = 4
MESH = pl.DeviceIdType.MESH


def remote(src, dst, send_sem, recv_sem, where):
    return pltpu.make_async_remote_copy(
        src_ref=src,
        dst_ref=dst,
        send_sem=send_sem,
        recv_sem=recv_sem,
        device_id=where,
        device_id_type=MESH,
    )


def paired(e, d, ne):
    other, bit = jnp.int32(0), 1
    while bit < ne:
        ours, step = lax.rem(lax.div(e, bit), 2), lax.rem(lax.div(d, bit), 2)
        other = other + lax.rem(ours + step, 2) * bit
        bit *= 2
    return other


def exchange_kernel(
    ng,
    ne,
    src_any,
    tgt_any,
    mpo_any,
    sec_any,
    column_any,
    wave_ref,
    left_any,
    right_any,
    gathered_ref,
    tiles_ref,
    right_ref,
    rest_ref,
    src_far,
    tgt_far,
    mpo_far,
    sec_far,
    slots_ref,
    outgoing,
    left_ref,
    src_ref,
    tgt_ref,
    mpo_ref,
    sec_ref,
    column_ref,
    src_two,
    tgt_two,
    mpo_two,
    sec_two,
    a2a_send,
    a2a_recv,
    fwd_send,
    fwd_recv,
    ag_send,
    ag_recv,
    agf_send,
    agf_recv,
    own_send,
    own_recv,
    local_sem,
):
    g = lax.axis_index("grp")
    e = lax.axis_index("env")
    chips = ng // 2
    core = lax.rem(g, 2)
    chip = lax.div(g, 2)
    partner = chip * 2 + 1 - core

    def mate(d):
        return paired(e, d, ne)

    tiles_dev = left_ref.shape[0]
    top = outgoing.shape[2]
    bpd = wave_ref.shape[0]

    starts = (
        (sec_any, sec_ref),
        (column_any, column_ref),
        (left_any, left_ref),
        (src_any, src_ref),
        (tgt_any, tgt_ref),
        (mpo_any, mpo_ref),
        (right_any, right_ref),
    )
    loads = [
        pltpu.make_async_copy(a, b, local_sem.at[6 + i]) for i, (a, b) in enumerate(starts)
    ]
    for load in loads[:3]:
        load.start()

    barrier = pltpu.get_barrier_semaphore()

    def greet_env(d, c):
        pl.semaphore_signal(
            barrier, inc=1, device_id={"grp": g, "env": mate(d)}, device_id_type=MESH
        )
        return c

    def greet_chip(d, c):
        pl.semaphore_signal(
            barrier,
            inc=1,
            device_id={"grp": lax.rem(chip + d, chips) * 2 + core, "env": e},
            device_id_type=MESH,
        )
        return c

    lax.fori_loop(1, ne, greet_env, 0)
    lax.fori_loop(1, chips, greet_chip, 0)
    pl.semaphore_signal(barrier, inc=1, device_id={"grp": partner, "env": e}, device_id_type=MESH)

    def ranked(read, wanted):
        packed, weight, count = jnp.int32(0), jnp.int32(1), jnp.int32(0)
        for t in range(tiles_dev):
            hit = read(t) == wanted
            packed = packed + jnp.where(hit, t * weight, 0)
            weight = jnp.where(hit, weight * tiles_dev, weight)
            count = count + jnp.where(hit, 1, 0)
        picks = []
        for s in range(MAXS):
            picks.append(lax.rem(packed, tiles_dev))
            packed = lax.div(packed, tiles_dev)
        return picks, count

    def choose(c, carry):
        base = e * tiles_dev
        picks, _ = ranked(lambda t: sec_ref[base + t], column_ref[c])
        for s in range(MAXS):
            outgoing[c, s] = left_ref[picks[s], :top]
            rest_ref[c, s] = left_ref[picks[s], top:]
        return carry

    for load in loads[:3]:
        load.wait()
    lax.fori_loop(0, ne, choose, 0)

    pl.semaphore_wait(barrier, ne - 1 + chips)

    there = {"grp": partner, "env": e}

    def a2a(d):
        return remote(
            outgoing.at[mate(d)],
            tiles_ref.at[0, e],
            a2a_send.at[d],
            a2a_recv.at[d],
            {"grp": g, "env": mate(d)},
        )

    def a2a_in(d):
        src = mate(d)
        return remote(
            outgoing.at[src],
            tiles_ref.at[0, src],
            a2a_send.at[d],
            a2a_recv.at[d],
            {"grp": g, "env": mate(d)},
        )

    def forward(d):
        src = mate(d)
        return remote(
            tiles_ref.at[0, src], tiles_ref.at[1, src], fwd_send.at[d], fwd_recv.at[d], there
        )

    def ag(d):
        return remote(
            wave_ref,
            gathered_ref.at[g],
            ag_send.at[d],
            ag_recv.at[d],
            {"grp": lax.rem(chip + d, chips) * 2 + core, "env": e},
        )

    def ag_in(d):
        src = lax.rem(chip + chips - d, chips) * 2 + core
        return remote(
            wave_ref,
            gathered_ref.at[src],
            ag_send.at[d],
            ag_recv.at[d],
            {"grp": lax.rem(chip + d, chips) * 2 + core, "env": e},
        )

    def ag_forward(d):
        src = lax.rem(chip + chips - d, chips) * 2 + core
        return remote(
            gathered_ref.at[src], gathered_ref.at[src], agf_send.at[d], agf_recv.at[d], there
        )

    def ag_forward_in(d):
        src = lax.rem(chip + chips - d, chips) * 2 + 1 - core
        return remote(
            gathered_ref.at[src], gathered_ref.at[src], agf_send.at[d], agf_recv.at[d], there
        )

    def loop(low, high, act):
        def step(d, c):
            act(d)
            return c

        lax.fori_loop(low, high, step, 0)

    loop(1, ne, lambda d: a2a(d).start())
    loop(1, chips, lambda d: ag(d).start())
    far = (src_far, tgt_far, mpo_far, sec_far)
    own_meta = [
        remote(mine, theirs, own_send.at[3 + i], own_recv.at[3 + i], there)
        for i, (mine, theirs) in enumerate(zip((src_any, tgt_any, mpo_any, sec_any), far))
    ]
    for copy in own_meta:
        copy.start()
    own_wave = remote(wave_ref, gathered_ref.at[g], own_send.at[1], own_recv.at[1], there)
    own_wave.start()
    own_wave_in = remote(wave_ref, gathered_ref.at[partner], own_send.at[1], own_recv.at[1], there)
    own_tiles = remote(
        outgoing.at[e], tiles_ref.at[1, e], own_send.at[2], own_recv.at[2], there
    )
    own_tiles.start()
    keep_wave = pltpu.make_async_copy(wave_ref, gathered_ref.at[g], local_sem.at[0])
    keep_wave.start()
    keep_tiles = pltpu.make_async_copy(outgoing.at[e], tiles_ref.at[0, e], local_sem.at[1])
    keep_tiles.start()

    for load in loads[3:]:
        load.start()
    two = (src_two, tgt_two, mpo_two, sec_two)
    fetches = []
    for i in range(4):
        own_meta[i].wait_recv()
        fetches.append(pltpu.make_async_copy(far[i], two[i], local_sem.at[2 + i]))
        fetches[i].start()
    for fetch in fetches:
        fetch.wait()
    for load in loads[3:6]:
        load.wait()
    wanted = column_ref[e]

    def list_slots(half, source, goal, mpo, sector):
        def block(b, carry):
            base = b * tiles_dev
            picks, count = ranked(lambda t: sector[base + t], wanted)
            for s in range(MAXS):
                term = base + picks[s]
                target = goal[term]
                owner = lax.div(target, bpd)
                row = lax.rem(lax.div(owner, 2) + chips - chip, chips) * bpd + lax.rem(target, bpd)
                mine = (lax.rem(owner, 2) == core) & (count > s)
                place = (half * ne + b) * MAXS + s
                slots_ref[0, place] = jnp.where(mine, row, -1)
                slots_ref[1, place] = source[term]
                slots_ref[2, place] = mpo[term]
            return carry

        lax.fori_loop(0, ne, block, 0)

    list_slots(0, src_ref, tgt_ref, mpo_ref, sec_ref)
    list_slots(1, *two)

    def pass_on(d):
        a2a_in(d).wait_recv()
        forward(d).start()

    def pass_wave(d):
        ag_in(d).wait_recv()
        ag_forward(d).start()

    half = 1 + ne // 2
    loop(1, half, pass_on)
    loop(1, chips, pass_wave)
    loop(half, ne, pass_on)

    loop(1, ne, lambda d: forward(d).wait_recv())
    loop(1, chips, lambda d: ag_forward_in(d).wait_recv())
    own_wave_in.wait_recv()
    own_tiles.wait_recv()
    keep_wave.wait()
    loads[6].wait()
    keep_tiles.wait()
    loop(1, ne, lambda d: a2a(d).wait_send())
    loop(1, ne, lambda d: forward(d).wait_send())
    loop(1, chips, lambda d: ag(d).wait_send())
    loop(1, chips, lambda d: ag_forward(d).wait_send())
    for copy in own_meta:
        copy.wait_send()
    own_wave.wait_send()
    own_tiles.wait_send()


UNROLL = 4


def term_kernel(slots_ref, gathered_ref, tiles_ref, right_ref, own_ref, away_ref, total, listed):
    here = own_ref.shape[0]
    rows = here + away_ref.shape[0]
    places = slots_ref.shape[1]
    total[...] = jnp.zeros_like(total)

    def collect(i, n):
        row = slots_ref[0, i]
        listed[0, n] = row
        listed[1, n] = slots_ref[1, i]
        listed[2, n] = slots_ref[2, i]
        listed[3, n] = i
        return n + jnp.where(row >= 0, 1, 0)

    n = lax.fori_loop(0, places, collect, jnp.int32(0))
    for u in range(UNROLL):
        listed[0, n + u] = rows
        listed[1, n + u] = 0
        listed[2, n + u] = 0
        listed[3, n + u] = 0

    def batch(i, carry):
        images = []
        for u in range(UNROLL):
            at = i * UNROLL + u
            product = jnp.dot(
                tiles_ref[listed[3, at]],
                gathered_ref[listed[1, at]],
                preferred_element_type=jnp.float32,
            ).astype(jnp.bfloat16)
            images.append(
                jnp.dot(product, right_ref[listed[2, at]], preferred_element_type=jnp.float32)
            )
        for u in range(UNROLL):
            row = listed[0, i * UNROLL + u]
            total[row] = total[row] + images[u]
        return carry

    lax.fori_loop(0, lax.div(n + UNROLL - 1, UNROLL), batch, 0)

    def keep(r, carry):
        own_ref[r] = total[r].astype(own_ref.dtype)
        return carry

    def hand_out(r, carry):
        away_ref[r] = total[here + r].astype(away_ref.dtype)
        return carry

    lax.fori_loop(0, here, keep, 0)
    lax.fori_loop(0, rows - here, hand_out, 0)


def second_kernel(
    ng,
    ne,
    outgoing,
    away_ref,
    tiles_ref,
    landed_ref,
    a2a_send,
    a2a_recv,
    fwd_send,
    fwd_recv,
    sum_send,
    sum_recv,
    own_send,
    own_recv,
    local_sem,
):
    g = lax.axis_index("grp")
    e = lax.axis_index("env")
    chips = ng // 2
    core = lax.rem(g, 2)
    chip = lax.div(g, 2)
    partner = {"grp": chip * 2 + 1 - core, "env": e}

    def across(d):
        return {"grp": lax.rem(chip + d, chips) * 2 + core, "env": e}

    def aside(d):
        return {"grp": g, "env": paired(e, d, ne)}

    def loop(low, high, act):
        def step(d, c):
            act(d)
            return c

        lax.fori_loop(low, high, step, 0)

    barrier = pltpu.get_barrier_semaphore()

    def greet(where):
        pl.semaphore_signal(barrier, inc=1, device_id=where, device_id_type=MESH)

    loop(1, ne, lambda d: greet(aside(d)))
    loop(1, chips, lambda d: greet(across(d)))
    greet(partner)
    pl.semaphore_wait(barrier, ne - 1 + chips)

    def a2a(d):
        return remote(
            outgoing.at[paired(e, d, ne)],
            tiles_ref.at[0, e],
            a2a_send.at[d],
            a2a_recv.at[d],
            aside(d),
        )

    def a2a_in(d):
        src = paired(e, d, ne)
        return remote(
            outgoing.at[src], tiles_ref.at[0, src], a2a_send.at[d], a2a_recv.at[d], aside(d)
        )

    def forward(d):
        src = paired(e, d, ne)
        return remote(
            tiles_ref.at[0, src], tiles_ref.at[1, src], fwd_send.at[d], fwd_recv.at[d], partner
        )

    def move(d):
        return remote(
            away_ref.at[d - 1], landed_ref.at[d - 1], sum_send.at[d], sum_recv.at[d], across(d)
        )

    loop(1, ne, lambda d: a2a(d).start())
    loop(1, chips, lambda d: move(d).start())
    own_tiles = remote(
        outgoing.at[e], tiles_ref.at[1, e], own_send.at[0], own_recv.at[0], partner
    )
    own_tiles.start()
    keep_tiles = pltpu.make_async_copy(outgoing.at[e], tiles_ref.at[0, e], local_sem.at[0])
    keep_tiles.start()

    def pass_on(d):
        a2a_in(d).wait_recv()
        forward(d).start()

    loop(1, ne, pass_on)
    loop(1, ne, lambda d: forward(d).wait_recv())
    loop(1, chips, lambda d: move(d).wait_recv())
    own_tiles.wait_recv()
    keep_tiles.wait()
    loop(1, ne, lambda d: a2a(d).wait_send())
    loop(1, ne, lambda d: forward(d).wait_send())
    loop(1, chips, lambda d: move(d).wait_send())
    own_tiles.wait_send()


def reduce_kernel(ng, away_ref, landed_ref, send_sem, recv_sem):
    g = lax.axis_index("grp")
    e = lax.axis_index("env")
    chips = ng // 2
    core = lax.rem(g, 2)
    chip = lax.div(g, 2)

    def there(d):
        return {"grp": lax.rem(chip + d, chips) * 2 + core, "env": e}

    barrier = pltpu.get_barrier_semaphore()
    for d in range(1, chips):
        pl.semaphore_signal(barrier, inc=1, device_id=there(d), device_id_type=MESH)
    pl.semaphore_wait(barrier, chips - 1)

    moves = [
        remote(
            away_ref.at[d - 1], landed_ref.at[d - 1], send_sem.at[d], recv_sem.at[d], there(d)
        )
        for d in range(1, chips)
    ]
    for move in moves:
        move.start()
    for move in moves:
        move.wait_recv()
    for move in moves:
        move.wait_send()


def combine_kernel(own_top, landed_top, own_low, landed_low, out_ref):
    top = own_top.shape[1]

    def total(own, landed, r):
        summed = own[r].astype(jnp.float32)
        for d in range(landed.shape[0]):
            summed = summed + landed[d, r].astype(jnp.float32)
        return summed.astype(out_ref.dtype)

    def block(r, carry):
        out_ref[r, :top] = total(own_top, landed_top, r)
        out_ref[r, top:] = total(own_low, landed_low, r)
        return carry

    lax.fori_loop(0, out_ref.shape[0], block, 0)


def shards(
    wavefunction,
    left_tiles,
    right_tiles,
    term_source,
    term_target,
    right_index,
    term_sector,
    column_sector,
):
    tile = left_tiles.shape[1]
    tiles_dev = left_tiles.shape[0]
    ne = lax.axis_size("env")
    ng = lax.axis_size("grp")
    chips = ng // 2
    rows_dev = wavefunction.shape[0]
    bpd = rows_dev // tile
    meta = (term_source, term_target, right_index, term_sector[:, 0])
    listing = jax.ShapeDtypeStruct(term_source.shape, jnp.int32)
    tile_bytes = tile * tile * 2
    spare = 4 << 20
    wave = wavefunction.reshape(bpd, tile, tile)
    bf16 = jnp.bfloat16
    vmem = pl.BlockSpec(memory_space=pltpu.VMEM)
    smem = pl.BlockSpec(memory_space=pltpu.SMEM)
    hbm = pl.BlockSpec(memory_space=pltpu.HBM)
    anywhere = pl.BlockSpec(memory_space=pl.ANY)
    places = 2 * ne * MAXS
    dma = pltpu.SemaphoreType.DMA

    operands = (*meta, column_sector, wave, left_tiles, right_tiles)
    top = tile // 2
    low = tile - top
    gathered, tiles, right_held, rest, *_, slots = pl.pallas_call(
        functools.partial(exchange_kernel, ng, ne),
        out_shape=(
            jax.ShapeDtypeStruct((ng, bpd, tile, tile), bf16),
            jax.ShapeDtypeStruct((2, ne, MAXS, top, tile), bf16),
            jax.ShapeDtypeStruct(right_tiles.shape, bf16),
            jax.ShapeDtypeStruct((ne, MAXS, low, tile), bf16),
            listing,
            listing,
            listing,
            listing,
            jax.ShapeDtypeStruct((3, places), jnp.int32),
        ),
        in_specs=[hbm] * 8,
        out_specs=(anywhere,) * 3 + (vmem,) + (anywhere,) * 4 + (smem,),
        scratch_shapes=[
            pltpu.VMEM((ne, MAXS, top, tile), bf16),
            pltpu.VMEM(left_tiles.shape, bf16),
            *[pltpu.SMEM(listing.shape, jnp.int32) for _ in range(4)],
            pltpu.SMEM(column_sector.shape, jnp.int32),
            *[pltpu.SMEM(listing.shape, jnp.int32) for _ in range(4)],
            dma((ne,)),
            dma((ne,)),
            dma((ne,)),
            dma((ne,)),
            dma((chips,)),
            dma((chips,)),
            dma((chips,)),
            dma((chips,)),
            dma((7,)),
            dma((7,)),
            dma((13,)),
        ],
        compiler_params=pltpu.CompilerParams(
            collective_id=0,
            has_side_effects=True,
            vmem_limit_bytes=spare + tile_bytes * (tiles_dev + ne * MAXS),
        ),
        name="exchange",
    )(*[pltpu.with_memory_space_constraint(a, pltpu.HBM) for a in operands])

    waves = gathered.reshape(ng * bpd, tile, tile)

    def contribute(tiles, span):
        return pl.pallas_call(
            term_kernel,
            out_shape=(
                jax.ShapeDtypeStruct((bpd, span, tile), bf16),
                jax.ShapeDtypeStruct(((chips - 1) * bpd, span, tile), bf16),
            ),
            in_specs=[smem, vmem, vmem, vmem],
            out_specs=(vmem, vmem),
            scratch_shapes=[
                pltpu.VMEM((chips * bpd + 1, span, tile), jnp.float32),
                pltpu.SMEM((4, places + UNROLL), jnp.int32),
            ],
            compiler_params=pltpu.CompilerParams(
                vmem_limit_bytes=spare
                + tile_bytes * (ng * bpd + places + right_tiles.shape[0] + 3 * chips * bpd + 2)
            ),
            name="terms",
        )(slots, waves, tiles.reshape(places, span, tile), right_held)

    own_top, away_top = contribute(tiles, top)
    low_tiles, landed_top = pl.pallas_call(
        functools.partial(second_kernel, ng, ne),
        out_shape=(
            jax.ShapeDtypeStruct((2, ne, MAXS, low, tile), bf16),
            jax.ShapeDtypeStruct((chips - 1, bpd * top, tile), bf16),
        ),
        in_specs=[anywhere, anywhere],
        out_specs=(anywhere, anywhere),
        scratch_shapes=[
            *[dma((ne,)) for _ in range(4)],
            dma((chips,)),
            dma((chips,)),
            dma((1,)),
            dma((1,)),
            dma((1,)),
        ],
        compiler_params=pltpu.CompilerParams(
            collective_id=2, has_side_effects=True, vmem_limit_bytes=spare
        ),
        name="second",
    )(rest, away_top.reshape(chips - 1, bpd * top, tile))

    own_low, away_low = contribute(low_tiles, low)
    landed_low = pl.pallas_call(
        functools.partial(reduce_kernel, ng),
        out_shape=jax.ShapeDtypeStruct((chips - 1, bpd * low, tile), bf16),
        in_specs=[anywhere],
        out_specs=anywhere,
        scratch_shapes=[dma((chips,)), dma((chips,))],
        compiler_params=pltpu.CompilerParams(
            collective_id=1, has_side_effects=True, vmem_limit_bytes=spare
        ),
        name="reduce",
    )(away_low.reshape(chips - 1, bpd * low, tile))
    summed = pl.pallas_call(
        combine_kernel,
        out_shape=jax.ShapeDtypeStruct((bpd, tile, tile), bf16),
        in_specs=[vmem] * 4,
        out_specs=vmem,
        compiler_params=pltpu.CompilerParams(
            vmem_limit_bytes=spare + tile_bytes * bpd * (chips + 1)
        ),
        name="combine",
    )(
        own_top,
        landed_top.reshape(chips - 1, bpd, top, tile),
        own_low,
        landed_low.reshape(chips - 1, bpd, low, tile),
    )
    return summed.reshape(rows_dev, tile)


def solution(mesh):
    placed = (
        P("grp", "env"),
        P(("grp", "env"), None, None),
        P(None, "env", None),
        P("grp"),
        P("grp"),
        P("grp"),
        P("grp", None),
        P(),
    )
    return jax.shard_map(
        shards, mesh=mesh, in_specs=placed, out_specs=P("grp", "env"), check_vma=False
    )
```

```python
import functools

import jax
import jax.numpy as jnp
from jax import lax
from jax.experimental import pallas as pl
from jax.experimental.pallas import tpu as pltpu
from jax.sharding import PartitionSpec as P

MAXS = 4
MESH = pl.DeviceIdType.MESH


def remote(src, dst, send_sem, recv_sem, where):
    return pltpu.make_async_remote_copy(
        src_ref=src,
        dst_ref=dst,
        send_sem=send_sem,
        recv_sem=recv_sem,
        device_id=where,
        device_id_type=MESH,
    )


def exchange_kernel(
    ng,
    ne,
    src_any,
    tgt_any,
    mpo_any,
    sec_any,
    column_any,
    wave_ref,
    left_any,
    right_any,
    gathered_ref,
    tiles_ref,
    right_ref,
    src_far,
    tgt_far,
    mpo_far,
    sec_far,
    slots_ref,
    outgoing,
    left_ref,
    src_ref,
    tgt_ref,
    mpo_ref,
    sec_ref,
    column_ref,
    src_two,
    tgt_two,
    mpo_two,
    sec_two,
    a2a_send,
    a2a_recv,
    fwd_send,
    fwd_recv,
    ag_send,
    ag_recv,
    agf_send,
    agf_recv,
    own_send,
    own_recv,
    local_sem,
):
    g = lax.axis_index("grp")
    e = lax.axis_index("env")
    chips = ng // 2
    core = lax.rem(g, 2)
    chip = lax.div(g, 2)
    partner = chip * 2 + 1 - core

    def mate(d):
        other, bit = jnp.int32(0), 1
        while bit < ne:
            ours, step = lax.rem(lax.div(e, bit), 2), lax.rem(lax.div(d, bit), 2)
            other = other + lax.rem(ours + step, 2) * bit
            bit *= 2
        return other

    tiles_dev = left_ref.shape[0]
    bpd = wave_ref.shape[0]

    starts = (
        (sec_any, sec_ref),
        (column_any, column_ref),
        (left_any, left_ref),
        (src_any, src_ref),
        (tgt_any, tgt_ref),
        (mpo_any, mpo_ref),
        (right_any, right_ref),
    )
    loads = [
        pltpu.make_async_copy(a, b, local_sem.at[6 + i]) for i, (a, b) in enumerate(starts)
    ]
    for load in loads[:3]:
        load.start()

    barrier = pltpu.get_barrier_semaphore()

    def greet_env(d, c):
        pl.semaphore_signal(
            barrier, inc=1, device_id={"grp": g, "env": mate(d)}, device_id_type=MESH
        )
        return c

    def greet_chip(d, c):
        pl.semaphore_signal(
            barrier,
            inc=1,
            device_id={"grp": lax.rem(chip + d, chips) * 2 + core, "env": e},
            device_id_type=MESH,
        )
        return c

    lax.fori_loop(1, ne, greet_env, 0)
    lax.fori_loop(1, chips, greet_chip, 0)
    pl.semaphore_signal(barrier, inc=1, device_id={"grp": partner, "env": e}, device_id_type=MESH)

    def ranked(read, wanted):
        packed, weight, count = jnp.int32(0), jnp.int32(1), jnp.int32(0)
        for t in range(tiles_dev):
            hit = read(t) == wanted
            packed = packed + jnp.where(hit, t * weight, 0)
            weight = jnp.where(hit, weight * tiles_dev, weight)
            count = count + jnp.where(hit, 1, 0)
        picks = []
        for s in range(MAXS):
            picks.append(lax.rem(packed, tiles_dev))
            packed = lax.div(packed, tiles_dev)
        return picks, count

    def choose(c, carry):
        base = e * tiles_dev
        picks, _ = ranked(lambda t: sec_ref[base + t], column_ref[c])
        for s in range(MAXS):
            outgoing[c, s] = left_ref[picks[s]]
        return carry

    for load in loads[:3]:
        load.wait()
    lax.fori_loop(0, ne, choose, 0, unroll=4 if ne % 4 == 0 else 1)

    pl.semaphore_wait(barrier, ne - 1 + chips)

    there = {"grp": partner, "env": e}

    def a2a(d):
        return remote(
            outgoing.at[mate(d)],
            tiles_ref.at[0, e],
            a2a_send.at[d],
            a2a_recv.at[d],
            {"grp": g, "env": mate(d)},
        )

    def a2a_in(d):
        src = mate(d)
        return remote(
            outgoing.at[src],
            tiles_ref.at[0, src],
            a2a_send.at[d],
            a2a_recv.at[d],
            {"grp": g, "env": mate(d)},
        )

    def forward(d):
        src = mate(d)
        return remote(
            tiles_ref.at[0, src], tiles_ref.at[1, src], fwd_send.at[d], fwd_recv.at[d], there
        )

    def ag(d):
        return remote(
            wave_ref,
            gathered_ref.at[g],
            ag_send.at[d],
            ag_recv.at[d],
            {"grp": lax.rem(chip + d, chips) * 2 + core, "env": e},
        )

    def ag_in(d):
        src = lax.rem(chip + chips - d, chips) * 2 + core
        return remote(
            wave_ref,
            gathered_ref.at[src],
            ag_send.at[d],
            ag_recv.at[d],
            {"grp": lax.rem(chip + d, chips) * 2 + core, "env": e},
        )

    def ag_forward(d):
        src = lax.rem(chip + chips - d, chips) * 2 + core
        return remote(
            gathered_ref.at[src], gathered_ref.at[src], agf_send.at[d], agf_recv.at[d], there
        )

    def ag_forward_in(d):
        src = lax.rem(chip + chips - d, chips) * 2 + 1 - core
        return remote(
            gathered_ref.at[src], gathered_ref.at[src], agf_send.at[d], agf_recv.at[d], there
        )

    def loop(low, high, act):
        def step(d, c):
            act(d)
            return c

        lax.fori_loop(low, high, step, 0)

    loop(1, ne, lambda d: a2a(d).start())
    loop(1, chips, lambda d: ag(d).start())
    far = (src_far, tgt_far, mpo_far, sec_far)
    own_meta = [
        remote(mine, theirs, own_send.at[3 + i], own_recv.at[3 + i], there)
        for i, (mine, theirs) in enumerate(zip((src_any, tgt_any, mpo_any, sec_any), far))
    ]
    for copy in own_meta:
        copy.start()
    own_wave = remote(wave_ref, gathered_ref.at[g], own_send.at[1], own_recv.at[1], there)
    own_wave.start()
    own_wave_in = remote(wave_ref, gathered_ref.at[partner], own_send.at[1], own_recv.at[1], there)
    own_tiles = remote(
        outgoing.at[e], tiles_ref.at[1, e], own_send.at[2], own_recv.at[2], there
    )
    own_tiles.start()
    keep_wave = pltpu.make_async_copy(wave_ref, gathered_ref.at[g], local_sem.at[0])
    keep_wave.start()
    keep_tiles = pltpu.make_async_copy(outgoing.at[e], tiles_ref.at[0, e], local_sem.at[1])
    keep_tiles.start()

    for load in loads[3:]:
        load.start()
    two = (src_two, tgt_two, mpo_two, sec_two)
    fetches = []
    for i in range(4):
        own_meta[i].wait_recv()
        fetches.append(pltpu.make_async_copy(far[i], two[i], local_sem.at[2 + i]))
        fetches[i].start()
    for fetch in fetches:
        fetch.wait()
    for load in loads[3:6]:
        load.wait()
    wanted = column_ref[e]

    def list_slots(half, source, goal, mpo, sector):
        def block(b, carry):
            base = b * tiles_dev
            picks, count = ranked(lambda t: sector[base + t], wanted)
            for s in range(MAXS):
                term = base + picks[s]
                target = goal[term]
                owner = lax.div(target, bpd)
                row = lax.rem(lax.div(owner, 2) + chips - chip, chips) * bpd + lax.rem(target, bpd)
                mine = (lax.rem(owner, 2) == core) & (count > s)
                place = (half * ne + b) * MAXS + s
                slots_ref[0, place] = jnp.where(mine, row, -1)
                slots_ref[1, place] = source[term]
                slots_ref[2, place] = mpo[term]
            return carry

        lax.fori_loop(0, ne, block, 0)

    list_slots(0, src_ref, tgt_ref, mpo_ref, sec_ref)
    list_slots(1, *two)

    def pass_on(d):
        a2a_in(d).wait_recv()
        forward(d).start()

    def pass_wave(d):
        ag_in(d).wait_recv()
        ag_forward(d).start()

    half = 1 + ne // 2
    loop(1, half, pass_on)
    loop(1, chips, pass_wave)
    loop(half, ne, pass_on)

    loop(1, ne, lambda d: forward(d).wait_recv())
    loop(1, chips, lambda d: ag_forward_in(d).wait_recv())
    own_wave_in.wait_recv()
    own_tiles.wait_recv()
    keep_wave.wait()
    loads[6].wait()
    keep_tiles.wait()
    loop(1, ne, lambda d: a2a(d).wait_send())
    loop(1, ne, lambda d: forward(d).wait_send())
    loop(1, chips, lambda d: ag(d).wait_send())
    loop(1, chips, lambda d: ag_forward(d).wait_send())
    for copy in own_meta:
        copy.wait_send()
    own_wave.wait_send()
    own_tiles.wait_send()


UNROLL = 8


def term_kernel(slots_ref, gathered_ref, tiles_ref, right_ref, own_ref, away_ref, total, listed):
    here = own_ref.shape[0]
    rows = here + away_ref.shape[0]
    places = slots_ref.shape[1]
    total[...] = jnp.zeros_like(total)

    def collect(i, n):
        row = slots_ref[0, i]
        listed[0, n] = row
        listed[1, n] = slots_ref[1, i]
        listed[2, n] = slots_ref[2, i]
        listed[3, n] = i
        return n + jnp.where(row >= 0, 1, 0)

    n = lax.fori_loop(0, places, collect, jnp.int32(0), unroll=4)
    for u in range(UNROLL):
        listed[0, n + u] = rows
        listed[1, n + u] = 0
        listed[2, n + u] = 0
        listed[3, n + u] = 0

    def batch(i, carry):
        images = []
        for u in range(UNROLL):
            at = i * UNROLL + u
            product = jnp.dot(
                tiles_ref[listed[3, at]],
                gathered_ref[listed[1, at]],
                preferred_element_type=jnp.float32,
            ).astype(jnp.bfloat16)
            images.append(
                jnp.dot(product, right_ref[listed[2, at]], preferred_element_type=jnp.float32)
            )
        for u in range(UNROLL):
            row = listed[0, i * UNROLL + u]
            total[row] = total[row] + images[u]
        return carry

    lax.fori_loop(0, lax.div(n + UNROLL - 1, UNROLL), batch, 0)

    def keep(r, carry):
        own_ref[r] = total[r].astype(own_ref.dtype)
        return carry

    def hand_out(r, carry):
        away_ref[r] = total[here + r].astype(away_ref.dtype)
        return carry

    lax.fori_loop(0, here, keep, 0, unroll=2)
    lax.fori_loop(0, rows - here, hand_out, 0, unroll=2)


def reduce_kernel(ng, away_ref, landed_ref, send_sem, recv_sem):
    g = lax.axis_index("grp")
    e = lax.axis_index("env")
    chips = ng // 2
    core = lax.rem(g, 2)
    chip = lax.div(g, 2)

    def there(d):
        return {"grp": lax.rem(chip + d, chips) * 2 + core, "env": e}

    barrier = pltpu.get_barrier_semaphore()
    for d in range(1, chips):
        pl.semaphore_signal(barrier, inc=1, device_id=there(d), device_id_type=MESH)
    pl.semaphore_wait(barrier, chips - 1)

    moves = [
        remote(
            away_ref.at[d - 1], landed_ref.at[d - 1], send_sem.at[d], recv_sem.at[d], there(d)
        )
        for d in range(1, chips)
    ]
    for move in moves:
        move.start()
    for move in moves:
        move.wait_recv()
    for move in moves:
        move.wait_send()


def shards(
    wavefunction,
    left_tiles,
    right_tiles,
    term_source,
    term_target,
    right_index,
    term_sector,
    column_sector,
):
    tile = left_tiles.shape[1]
    tiles_dev = left_tiles.shape[0]
    ne = lax.axis_size("env")
    ng = lax.axis_size("grp")
    chips = ng // 2
    rows_dev = wavefunction.shape[0]
    bpd = rows_dev // tile
    meta = (term_source, term_target, right_index, term_sector[:, 0])
    listing = jax.ShapeDtypeStruct(term_source.shape, jnp.int32)
    tile_bytes = tile * tile * 2
    spare = 4 << 20
    wave = wavefunction.reshape(bpd, tile, tile)
    bf16 = jnp.bfloat16
    vmem = pl.BlockSpec(memory_space=pltpu.VMEM)
    smem = pl.BlockSpec(memory_space=pltpu.SMEM)
    hbm = pl.BlockSpec(memory_space=pltpu.HBM)
    anywhere = pl.BlockSpec(memory_space=pl.ANY)
    places = 2 * ne * MAXS
    dma = pltpu.SemaphoreType.DMA

    operands = (*meta, column_sector, wave, left_tiles, right_tiles)
    gathered, tiles, right_held, *_, slots = pl.pallas_call(
        functools.partial(exchange_kernel, ng, ne),
        out_shape=(
            jax.ShapeDtypeStruct((ng, bpd, tile, tile), bf16),
            jax.ShapeDtypeStruct((2, ne, MAXS, tile, tile), bf16),
            jax.ShapeDtypeStruct(right_tiles.shape, bf16),
            listing,
            listing,
            listing,
            listing,
            jax.ShapeDtypeStruct((3, places), jnp.int32),
        ),
        in_specs=[hbm] * 8,
        out_specs=(anywhere,) * 7 + (smem,),
        scratch_shapes=[
            pltpu.VMEM((ne, MAXS, tile, tile), bf16),
            pltpu.VMEM(left_tiles.shape, bf16),
            *[pltpu.SMEM(listing.shape, jnp.int32) for _ in range(4)],
            pltpu.SMEM(column_sector.shape, jnp.int32),
            *[pltpu.SMEM(listing.shape, jnp.int32) for _ in range(4)],
            dma((ne,)),
            dma((ne,)),
            dma((ne,)),
            dma((ne,)),
            dma((chips,)),
            dma((chips,)),
            dma((chips,)),
            dma((chips,)),
            dma((7,)),
            dma((7,)),
            dma((13,)),
        ],
        compiler_params=pltpu.CompilerParams(
            collective_id=0,
            has_side_effects=True,
            vmem_limit_bytes=spare + tile_bytes * (tiles_dev + ne * MAXS),
        ),
        name="exchange",
    )(*[pltpu.with_memory_space_constraint(a, pltpu.HBM) for a in operands])

    own, away = pl.pallas_call(
        term_kernel,
        out_shape=(
            jax.ShapeDtypeStruct((bpd, tile, tile), bf16),
            jax.ShapeDtypeStruct(((chips - 1) * bpd, tile, tile), bf16),
        ),
        in_specs=[smem, vmem, vmem, vmem],
        out_specs=(vmem, vmem),
        scratch_shapes=[
            pltpu.VMEM((chips * bpd + 1, tile, tile), jnp.float32),
            pltpu.SMEM((4, places + UNROLL), jnp.int32),
        ],
        compiler_params=pltpu.CompilerParams(
            vmem_limit_bytes=spare
            + tile_bytes * (ng * bpd + places + right_tiles.shape[0] + 3 * chips * bpd + 2)
        ),
        name="terms",
    )(
        slots,
        gathered.reshape(ng * bpd, tile, tile),
        tiles.reshape(places, tile, tile),
        right_held,
    )

    landed = pl.pallas_call(
        functools.partial(reduce_kernel, ng),
        out_shape=jax.ShapeDtypeStruct((chips - 1, rows_dev, tile), bf16),
        in_specs=[anywhere],
        out_specs=anywhere,
        scratch_shapes=[dma((chips,)), dma((chips,))],
        compiler_params=pltpu.CompilerParams(
            collective_id=1, has_side_effects=True, vmem_limit_bytes=spare
        ),
        name="reduce",
    )(away.reshape(chips - 1, rows_dev, tile))
    summed = own.reshape(rows_dev, tile).astype(jnp.float32)
    for d in range(chips - 1):
        summed = summed + landed[d].astype(jnp.float32)
    return summed.astype(bf16)


def solution(mesh):
    placed = (
        P("grp", "env"),
        P(("grp", "env"), None, None),
        P(None, "env", None),
        P("grp"),
        P("grp"),
        P("grp"),
        P("grp", None),
        P(),
    )
    return jax.shard_map(
        shards, mesh=mesh, in_specs=placed, out_specs=P("grp", "env"), check_vma=False
    )
```
